32 devices in a mesh: seq: 8 (over y, x, core), chan: 4 (over z).
Axes of the slice: x: 2, y: 2, z: 4, core: 2. Of those that a mesh axis runs over, the one named last changes fastest.
Arguments:
- queries: bfloat16 [8192, 4096], P('seq', 'chan'), may hold values from -6 to 6
- key_input: bfloat16 [8192, 4096], P('seq', 'chan'), may hold values from -6 to 6
- value_input: bfloat16 [8192, 4096], P('seq', 'chan'), may hold values from -6 to 6
- basis_filters: bfloat16 [8192, 256], P('seq'), may hold values from -0.0625 to 0.0625
- tucker_factor: bfloat16 [4096, 256], P('chan'), may hold values from -0.375 to 0.375
- skip_bias: float32 [4096], P('chan'), may hold values from -4 to 4
- cotangent: bfloat16 [8192, 4096], P('seq', 'chan'), may hold values from -6 to 6
Outputs:
- hyena_out: bfloat16 [8192, 4096], P('seq', 'chan')
- grad_query: bfloat16 [8192, 4096], P('seq', 'chan')
- grad_key: bfloat16 [8192, 4096], P('seq', 'chan')
- grad_value: bfloat16 [8192, 4096], P('seq', 'chan')
- grad_factor: float32 [4096, 256], P('chan')
- grad_basis: float32 [8192, 256], P('seq')
The draws below stay inside these ranges and needn't reach their ends.
All inputs are finite; a program needn't handle non-finite values.
Results may differ from the reference program's by a relative error of at most 0.017.
Values may be sent and summed in bfloat16 or wider, within the bound.
A program may use at most 320 MiB of HBM per device.

```python
import jax
import jax.numpy as jnp
from jax import lax

D = 4096
BASIS = 256
SEQ_LEN = 8192


def level_of(own_key, shape, split, smallest, high):
    factor_of, own = 1.0, jax.random.fold_in(own_key, 6)
    for position, parts in split:
        draws = jnp.exp(jax.random.uniform(jax.random.fold_in(own, position), (parts,), jnp.float32, smallest / len(split), high / len(split)))
        factor_of = factor_of * jnp.repeat(draws, shape[position] // parts).reshape([-1 if axis == position else 1 for axis in range(len(shape))])
    return factor_of


def noise(own_key, dims, deviation, reach, pieces=(), held_as=jnp.bfloat16):
    drawn = jax.random.normal(own_key, dims, jnp.float32) * deviation
    if len(pieces) > 0:
        drawn = level_of(own_key, dims, pieces, -0.22, 0.18) * drawn
    return jnp.clip(drawn, min=-reach, max=reach).astype(held_as)


def setup_inputs(seed: int = 0) -> dict:
    key_of = jax.random.split(jax.random.key(seed), 8)
    return {
        "queries": noise(key_of[0], (SEQ_LEN, D), 1.0, 6.0, ((0, 8), (1, 4))),
        "key_input": noise(key_of[1], (SEQ_LEN, D), 1.0, 6.0, ((0, 8), (1, 4))),
        "value_input": noise(key_of[2], (SEQ_LEN, D), 1.0, 6.0, ((0, 8), (1, 4))),
        "basis_filters": noise(key_of[3], (SEQ_LEN, BASIS), SEQ_LEN ** -0.5, 0.0625, ((0, 8),)),
        "tucker_factor": noise(key_of[4], (D, BASIS), BASIS ** -0.5, 0.375, ((0, 4),)),
        "skip_bias": noise(key_of[5], (D,), 1.0, 4.0, ((0, 4),), jnp.float32),
        "cotangent": noise(key_of[6], (SEQ_LEN, D), 1.0, 6.0, ((0, 8), (1, 4))),
    }


def spectral_block(operands):
    mixed_in, gated_grad, filter_taps = operands
    length = mixed_in.shape[0]
    padded_size = 2 * length
    mixed_freq = jnp.fft.rfft(mixed_in.astype(jnp.float32), n=padded_size, axis=0)
    gated_freq = jnp.fft.rfft(gated_grad.astype(jnp.float32), n=padded_size, axis=0)
    filter_freq = jnp.fft.rfft(filter_taps.astype(jnp.float32), n=padded_size, axis=0)
    conv_out = jnp.fft.irfft(filter_freq * mixed_freq, n=padded_size, axis=0)[:length]
    conv_grad = jnp.fft.irfft(jnp.conj(filter_freq) * gated_freq, n=padded_size, axis=0)[:length]
    filter_grad = jnp.fft.irfft(jnp.conj(mixed_freq) * gated_freq, n=padded_size, axis=0)[:length]
    return conv_out.astype(jnp.bfloat16), conv_grad.astype(jnp.bfloat16), filter_grad.astype(jnp.bfloat16)


def reference(queries, key_input, value_input, basis_filters, tucker_factor, skip_bias, cotangent):
    length = queries.shape[0]
    model_width = queries.shape[1]
    block_width = min(model_width, 256)
    block_count = model_width // block_width
    grad_scale = length ** -0.5
    mixed_in = (key_input.astype(jnp.float32) * value_input.astype(jnp.float32)).astype(jnp.bfloat16)
    mixed_in = lax.optimization_barrier(mixed_in)
    gated_grad = (cotangent.astype(jnp.float32) * queries.astype(jnp.float32)).astype(jnp.bfloat16)
    gated_grad = lax.optimization_barrier(gated_grad)
    filter_taps = jnp.dot(basis_filters, tucker_factor.T, preferred_element_type=jnp.float32).astype(jnp.bfloat16)

    def split_cols(matrix):
        return jnp.transpose(matrix.reshape(length, block_count, block_width), (1, 0, 2))

    def join_cols(matrix):
        return jnp.transpose(matrix, (1, 0, 2)).reshape(length, model_width)

    conv_out, conv_grad, filter_grad = lax.map(
        spectral_block, (split_cols(mixed_in), split_cols(gated_grad), split_cols(filter_taps)))
    conv_out = join_cols(conv_out)
    conv_grad = join_cols(conv_grad)
    filter_grad = join_cols(filter_grad)
    pre_gate = conv_out.astype(jnp.float32) + skip_bias * mixed_in.astype(jnp.float32)
    hyena_out = (queries.astype(jnp.float32) * pre_gate).astype(jnp.bfloat16)
    grad_query = (cotangent.astype(jnp.float32) * pre_gate).astype(jnp.bfloat16)
    grad_mixed = conv_grad.astype(jnp.float32) + skip_bias * gated_grad.astype(jnp.float32)
    grad_key = (grad_mixed * value_input.astype(jnp.float32)).astype(jnp.bfloat16)
    grad_value = (grad_mixed * key_input.astype(jnp.float32)).astype(jnp.bfloat16)
    grad_factor = jnp.dot(filter_grad.T, basis_filters, preferred_element_type=jnp.float32) * grad_scale
    grad_basis = jnp.dot(filter_grad, tucker_factor, preferred_element_type=jnp.float32) * grad_scale
    return (hyena_out, grad_query, grad_key, grad_value, grad_factor, grad_basis)
```

```python
import math

import jax
import jax.numpy as jnp
from jax import lax
from jax.experimental import pallas as pl
from jax.experimental.pallas import tpu as pltpu
from jax.sharding import PartitionSpec as P

ACCURATE = lax.Precision.HIGH


def split_length(length):
    padded_size = 2 * length
    inner_size = 1
    for candidate in range(1, length + 1):
        if candidate * candidate > padded_size:
            break
        if length % candidate == 0:
            inner_size = candidate
    return (inner_size, padded_size // inner_size)


def phase_table(rows_count, cols_count, period):
    row_index = jnp.arange(rows_count, dtype=jnp.int32)[:, None]
    col_index = jnp.arange(cols_count, dtype=jnp.int32)[None, :]
    product = row_index * col_index % period
    angles = product.astype(jnp.float32) * (2.0 * math.pi / period)
    return (jnp.cos(angles), -jnp.sin(angles))


def make_tables(length):
    inner_size, outer_size = split_length(length)
    cosine_inner, sine_inner = phase_table(inner_size, inner_size, inner_size)
    cosine_outer, sine_outer = phase_table(outer_size, outer_size, outer_size)
    cosine_twist, sine_twist = phase_table(outer_size, inner_size, 2 * length)
    return (cosine_inner, sine_inner, cosine_outer, sine_outer, cosine_twist, sine_twist)


def table_product(table, blocks):
    high_part = table.astype(jnp.bfloat16)
    low_part = (table - high_part.astype(jnp.float32)).astype(jnp.bfloat16)
    return jnp.einsum(
        "kn,cna->cka", high_part, blocks, preferred_element_type=jnp.float32
    ) + jnp.einsum("kn,cna->cka", low_part, blocks, preferred_element_type=jnp.float32)


def forward_real(signal, tables):
    cosine_inner, sine_inner, cosine_outer, sine_outer, cosine_twist, sine_twist = tables
    inner_size = cosine_inner.shape[0]
    outer_half = cosine_outer.shape[0] // 2
    blocks = signal.reshape(signal.shape[0], outer_half, inner_size)
    section_real = table_product(cosine_outer[:, :outer_half], blocks)
    section_imag = table_product(sine_outer[:, :outer_half], blocks)
    twist_real = section_real * cosine_twist - section_imag * sine_twist
    twist_imag = section_real * sine_twist + section_imag * cosine_twist
    spectrum_real = jnp.einsum(
        "cka,ja->ckj", twist_real, cosine_inner, precision=ACCURATE
    ) - jnp.einsum("cka,ja->ckj", twist_imag, sine_inner, precision=ACCURATE)
    spectrum_imag = jnp.einsum(
        "cka,ja->ckj", twist_real, sine_inner, precision=ACCURATE
    ) + jnp.einsum("cka,ja->ckj", twist_imag, cosine_inner, precision=ACCURATE)
    return (spectrum_real, spectrum_imag)


def inverse_real(spectrum_real, spectrum_imag, tables):
    cosine_inner, sine_inner, cosine_outer, sine_outer, cosine_twist, sine_twist = tables
    inner_size = cosine_inner.shape[0]
    outer_half = cosine_outer.shape[0] // 2
    section_real = jnp.einsum(
        "ckj,aj->cka", spectrum_real, cosine_inner, precision=ACCURATE
    ) + jnp.einsum("ckj,aj->cka", spectrum_imag, sine_inner, precision=ACCURATE)
    section_imag = jnp.einsum(
        "ckj,aj->cka", spectrum_imag, cosine_inner, precision=ACCURATE
    ) - jnp.einsum("ckj,aj->cka", spectrum_real, sine_inner, precision=ACCURATE)
    twist_real = section_real * cosine_twist + section_imag * sine_twist
    twist_imag = section_imag * cosine_twist - section_real * sine_twist
    signal = jnp.einsum(
        "nk,cka->cna", cosine_outer[:outer_half], twist_real, precision=ACCURATE
    ) + jnp.einsum("nk,cka->cna", sine_outer[:outer_half], twist_imag, precision=ACCURATE)
    padded_size = cosine_outer.shape[0] * inner_size
    return (signal / padded_size).reshape(signal.shape[0], outer_half * inner_size)


def convolve(mixed_chan, gated_chan, filter_chan, tables):
    stacked = jnp.concatenate((mixed_chan, gated_chan, filter_chan), 0)
    spectrum_real, spectrum_imag = forward_real(stacked, tables)
    mixed_real, gated_real, filter_real = jnp.split(spectrum_real, 3, 0)
    mixed_imag, gated_imag, filter_imag = jnp.split(spectrum_imag, 3, 0)
    output_real = filter_real * mixed_real - filter_imag * mixed_imag
    output_imag = filter_real * mixed_imag + filter_imag * mixed_real
    backward_real = filter_real * gated_real + filter_imag * gated_imag
    backward_imag = filter_real * gated_imag - filter_imag * gated_real
    kernel_real = mixed_real * gated_real + mixed_imag * gated_imag
    kernel_imag = mixed_real * gated_imag - mixed_imag * gated_real
    signals = inverse_real(
        jnp.concatenate((output_real, backward_real, kernel_real), 0),
        jnp.concatenate((output_imag, backward_imag, kernel_imag), 0),
        tables,
    )
    conv_out, conv_grad, filter_grad = jnp.split(signals.astype(jnp.bfloat16), 3, 0)
    return (conv_out, conv_grad, filter_grad)


LANES = 128


def split_table(table, axis):
    high_part = table.astype(jnp.bfloat16)
    low_part = (table - high_part.astype(jnp.float32)).astype(jnp.bfloat16)
    return jnp.concatenate((high_part, low_part), axis)


def angle_table(left, right, period):
    product = left[:, None] * right[None, :] % period
    return product.astype(jnp.float32) * (2.0 * math.pi / period)


def kernel_tables(length):
    half = length // LANES
    padded_size = 2 * length
    odd = 2 * jnp.arange(half, dtype=jnp.int32) + 1
    rows = jnp.arange(half, dtype=jnp.int32)
    lags = jnp.arange(LANES, dtype=jnp.int32)
    outer = angle_table(odd, rows, 4 * half)
    first = split_table(jnp.concatenate((jnp.cos(outer), -jnp.sin(outer)), 0), 1)
    last = jnp.concatenate((jnp.cos(outer), -jnp.sin(outer)), 0).T * (2.0 / padded_size)
    inner = angle_table(lags, lags, LANES)
    twist = angle_table(odd, lags, 2 * padded_size)
    return (
        first,
        split_table(last, 1),
        jnp.cos(inner),
        jnp.sin(inner),
        jnp.cos(twist)[:, None, :],
        jnp.sin(twist)[:, None, :],
    )


def conv_kernel(mixed, gated, taps, first, last, cosine, sine, tw_cos, tw_sin, *rest):
    outs, (held, spec) = rest[:3], rest[3:]
    sources = (mixed, gated, taps)
    half = mixed.shape[0] // LANES
    pitch = LANES + 8

    def widen(j, carry):
        for g in range(3):
            rows = sources[g][pl.ds(pl.multiple_of(j * LANES, LANES), LANES), :]
            held[g, pl.ds(pl.multiple_of(j * pitch, 8), LANES), :] = rows.astype(jnp.float32)
        return carry

    lax.fori_loop(0, half, widen, 0)
    first_table = first[...]

    def analyse(i, carry):
        for g in range(3):
            pair = jnp.concatenate(
                [held[g, pl.ds(2 * i + e, half, stride=pitch), :] for e in range(2)], 1
            ).astype(jnp.bfloat16)
            section = jnp.dot(
                first_table,
                jnp.concatenate((pair, pair), 0),
                preferred_element_type=jnp.float32,
            )
            for e in range(2):
                spec[g, pl.ds(2 * i + e, 2 * half, stride=pitch), :] = section[
                    :, e * LANES : (e + 1) * LANES
                ]
        return carry

    lax.fori_loop(0, LANES // 2, analyse, 0, unroll=2)

    def multiply(k, carry):
        real_rows = pl.ds(pl.multiple_of(k * pitch, 8), LANES)
        imag_rows = pl.ds(pl.multiple_of((half + k) * pitch, 8), LANES)
        real = cosine[...] * tw_cos[k] - sine[...] * tw_sin[k]
        imag = -(sine[...] * tw_cos[k] + cosine[...] * tw_sin[k])
        forward = jnp.concatenate(
            (jnp.concatenate((real, -imag), 1), jnp.concatenate((imag, real), 1)), 0
        ).astype(jnp.bfloat16)
        real, imag = real.T, imag.T
        backward = jnp.concatenate(
            (jnp.concatenate((real, imag), 1), jnp.concatenate((-imag, real), 1)), 0
        ).astype(jnp.bfloat16)
        section = jnp.concatenate(
            [
                jnp.concatenate((spec[g, real_rows, :], spec[g, imag_rows, :]), 0)
                for g in range(3)
            ],
            1,
        ).astype(jnp.bfloat16)
        spectrum = jnp.dot(forward, section, preferred_element_type=jnp.float32)
        mr, gr, fr = (spectrum[:LANES, g * LANES : (g + 1) * LANES] for g in range(3))
        mi, gi, fi = (spectrum[LANES:, g * LANES : (g + 1) * LANES] for g in range(3))
        product = jnp.concatenate(
            (
                jnp.concatenate((fr * mr - fi * mi, fr * gr + fi * gi, mr * gr + mi * gi), 1),
                jnp.concatenate((fr * mi + fi * mr, fr * gi - fi * gr, mr * gi - mi * gr), 1),
            ),
            0,
        ).astype(jnp.bfloat16)
        result = jnp.dot(backward, product, preferred_element_type=jnp.float32)
        for g in range(3):
            spec[g, real_rows, :] = result[:LANES, g * LANES : (g + 1) * LANES]
            spec[g, imag_rows, :] = result[LANES:, g * LANES : (g + 1) * LANES]
        return carry

    lax.fori_loop(0, half, multiply, 0, unroll=2)
    last_table = last[...]

    def synthesise(i, carry):
        for g in range(3):
            pair = jnp.concatenate(
                [spec[g, pl.ds(2 * i + e, 2 * half, stride=pitch), :] for e in range(2)], 1
            ).astype(jnp.bfloat16)
            signal = jnp.dot(
                last_table,
                jnp.concatenate((pair, pair), 0),
                preferred_element_type=jnp.float32,
            )
            for e in range(2):
                held[g, pl.ds(2 * i + e, half, stride=pitch), :] = signal[
                    :, e * LANES : (e + 1) * LANES
                ]
        return carry

    lax.fori_loop(0, LANES // 2, synthesise, 0, unroll=2)

    def narrow(j, carry):
        for g in range(3):
            rows = held[g, pl.ds(pl.multiple_of(j * pitch, 8), LANES), :]
            outs[g][pl.ds(pl.multiple_of(j * LANES, LANES), LANES), :] = rows.astype(jnp.bfloat16)
        return carry

    lax.fori_loop(0, half, narrow, 0)


def convolve_lanes(mixed, gated, taps):
    length = mixed.shape[0]
    half = length // LANES
    pitch = LANES + 8
    vmem = pl.BlockSpec(memory_space=pltpu.VMEM)
    return pl.pallas_call(
        conv_kernel,
        out_shape=[jax.ShapeDtypeStruct(mixed.shape, jnp.bfloat16)] * 3,
        in_specs=[vmem] * 9,
        out_specs=[vmem] * 3,
        scratch_shapes=[
            pltpu.VMEM((3, half * pitch, LANES), jnp.float32),
            pltpu.VMEM((3, 2 * half * pitch, LANES), jnp.float32),
        ],
        compiler_params=pltpu.CompilerParams(vmem_limit_bytes=60 * 1024 * 1024),
    )(mixed, gated, taps, *kernel_tables(length))


def convolve_any(mixed, gated, taps):
    length, chans = mixed.shape
    if chans == LANES and length == 64 * LANES:
        return convolve_lanes(mixed, gated, taps)
    outs = convolve(mixed.T, gated.T, taps.T, make_tables(length))
    return tuple(out.T for out in outs)


def to_blocks(matrix, count):
    rows, cols = matrix.shape
    return matrix.reshape(rows, count, cols // count).transpose(1, 0, 2)


def from_blocks(blocks):
    count, rows, cols = blocks.shape
    return blocks.transpose(1, 0, 2).reshape(rows, count * cols)


def body(queries, key_input, value_input, basis_filters, tucker_factor, skip_bias, cotangent):
    seq_count = lax.axis_size("seq")
    seq_rank = lax.axis_index("seq")
    seq_rows = queries.shape[0]
    length = seq_rows * seq_count
    grad_scale = length ** (-0.5)
    chan_local = queries.shape[1] // seq_count
    basis_all = lax.all_gather(basis_filters, "seq", axis=0, tiled=True)
    mixed_in = (key_input.astype(jnp.float32) * value_input.astype(jnp.float32)).astype(
        jnp.bfloat16
    )
    gated_grad = (cotangent.astype(jnp.float32) * queries.astype(jnp.float32)).astype(jnp.bfloat16)
    mixed_chan, gated_chan = (
        lax.all_to_all(to_blocks(signal, seq_count), "seq", split_axis=0, concat_axis=0).reshape(
            length, chan_local
        )
        for signal in (mixed_in, gated_grad)
    )
    factor_rows = lax.dynamic_slice_in_dim(tucker_factor, seq_rank * chan_local, chan_local, 0)
    filter_chan = lax.dot_general(
        basis_all, factor_rows, (((1,), (1,)), ((), ())), preferred_element_type=jnp.float32
    ).astype(jnp.bfloat16)
    conv_out, conv_grad, filter_grad = convolve_any(mixed_chan, gated_chan, filter_chan)
    basis_part = lax.psum_scatter(
        jnp.dot(filter_grad, factor_rows, preferred_element_type=jnp.float32).astype(jnp.bfloat16),
        "seq",
        scatter_dimension=0,
        tiled=True,
    )
    output_cols, backward_cols = (
        from_blocks(
            lax.all_to_all(
                signal.reshape(seq_count, seq_rows, chan_local), "seq", split_axis=0, concat_axis=0
            )
        )
        for signal in (conv_out, conv_grad)
    )
    factor_part = lax.dot_general(
        filter_grad, basis_all, (((0,), (0,)), ((), ())), preferred_element_type=jnp.float32
    )
    grad_factor = lax.all_gather(
        (factor_part * grad_scale).astype(jnp.bfloat16), "seq", axis=0, tiled=True
    ).astype(jnp.float32)
    grad_basis = lax.psum(basis_part, "chan").astype(jnp.float32) * grad_scale
    pre_gate = output_cols.astype(jnp.float32) + skip_bias * mixed_in.astype(jnp.float32)
    hyena_out = (queries.astype(jnp.float32) * pre_gate).astype(jnp.bfloat16)
    grad_query = (cotangent.astype(jnp.float32) * pre_gate).astype(jnp.bfloat16)
    grad_mixed = backward_cols.astype(jnp.float32) + skip_bias * gated_grad.astype(jnp.float32)
    grad_key = (grad_mixed * value_input.astype(jnp.float32)).astype(jnp.bfloat16)
    grad_value = (grad_mixed * key_input.astype(jnp.float32)).astype(jnp.bfloat16)
    return (hyena_out, grad_query, grad_key, grad_value, grad_factor, grad_basis)


def solution(mesh):
    return jax.shard_map(
        body,
        mesh=mesh,
        in_specs=(
            P("seq", "chan"),
            P("seq", "chan"),
            P("seq", "chan"),
            P("seq", None),
            P("chan", None),
            P("chan"),
            P("seq", "chan"),
        ),
        out_specs=(
            P("seq", "chan"),
            P("seq", "chan"),
            P("seq", "chan"),
            P("seq", "chan"),
            P("chan", None),
            P("seq", None),
        ),
        check_vma=False,
    )
```
